32 devices in a mesh: dp: 4 (over y, core), ctx: 8 (over z, x).
Axes of the slice: x: 2, y: 2, z: 4, core: 2. Of those that a mesh axis runs over, the one named last changes fastest.
Arguments:
- features: bfloat16 [4, 8, 248, 12288], P('dp', 'ctx'), may hold values from -6 to 6
- counts: int32 [4, 8], P('dp', 'ctx'), may hold values from 8 to 248, as said below
- short_taps: float32 [7, 3, 4096], P(None, None, 'ctx'), may hold values from -2 to 2
- residue: float32 [16, 256], P(None, 'ctx'), may hold values from -0.25 to 0.25
- decay_rate: float32 [16, 256], P(None, 'ctx'), may hold values from 1.953125e-05 to 0.05
- skip_gain: float32 [4096], P('ctx'), may hold values from -4 to 4
- cotangent: bfloat16 [4, 8, 248, 4096], P('dp', 'ctx'), may hold values from -6 to 6
Outputs:
- output: bfloat16 [4, 8, 248, 4096], P('dp', 'ctx')
- grad_features: bfloat16 [4, 8, 248, 12288], P('dp', 'ctx')
- grad_taps: float32 [7, 3, 4096], P(None, None, 'ctx')
- grad_residue: float32 [16, 256], P(None, 'ctx')
- grad_skip: float32 [4096], P('ctx')
The draws below stay inside these ranges and needn't reach their ends.
Inputs may be any that keep to these rules, and one draw needn't show every extreme that they name: Along ctx the loader shards come in pairs 2m, 2m + 1 whose counts sum to 256; each replica has a shard holding exactly 248 rows; the counts of a replica sum to 1024.
All inputs are finite; a program needn't handle non-finite values.
Results may differ from the reference program's by a relative error of at most 0.0069.
Values may be sent and summed in bfloat16 or wider, within the bound.
A program may use at most 128 MiB of HBM per device.

```python
import math
import jax
import jax.numpy as jnp
from jax import lax

D = 4096
GROUP = 16
FILTERS = 256
POLES = 16
TAPS = 7
TOK_DEV = 128
CAP = 248
N_DP = 4
N_CTX = 8


def draw_counts(key, part):
    pair_count = N_CTX // 2
    first_key, second_key, third_key = jax.random.split(key, 3)
    reach = TOK_DEV - 8
    offsets_pair = jax.random.randint(first_key, (N_DP, pair_count), -reach, reach + 1)
    chosen = jax.random.randint(second_key, (N_DP, 1), 0, pair_count)
    sign_draw = jax.random.randint(third_key, (N_DP, 1), 0, 2) * 2 - 1
    pair_ids = jnp.arange(pair_count)[None, :]
    offsets_pair = jnp.where(pair_ids == chosen, sign_draw * reach, offsets_pair)
    paired = jnp.stack([TOK_DEV + offsets_pair, TOK_DEV - offsets_pair], axis=-1)
    return paired.reshape(N_DP, N_CTX).astype(jnp.int32)


def level_of(rng, dims, cuts, low, largest):
    level = 1.0
    for position, blocks in cuts:
        heights = jax.random.uniform(jax.random.fold_in(jax.random.fold_in(rng, 6), position), (blocks,), jnp.float32, low / len(cuts), largest / len(cuts))
        level = level * jnp.repeat(jnp.exp(heights), dims[position] // blocks).reshape((-1,) + (1,) * (len(dims) - 1 - position))
    return level


def noise(key, shape, scale, most, shards=(), kind=jnp.bfloat16):
    values = jax.random.normal(key, shape, jnp.float32) * scale
    if len(shards) > 0:
        values = level_of(key, shape, shards, -0.22, 0.18) * values
    return jnp.clip(values, min=-most, max=most).astype(kind)


def setup_inputs(seed: int = 0) -> dict:
    keys = jax.random.split(jax.random.key(seed), 8)
    return {
        "features": noise(keys[0], (N_DP, N_CTX, CAP, 3 * D), 1.0, 6.0, ((0, 4), (1, 8))),
        "counts": draw_counts(jax.random.fold_in(keys[7], 71), 0),
        "short_taps": noise(keys[2], (TAPS, 3, D), TAPS ** -0.5, 2.0, ((2, 8),), jnp.float32),
        "residue": noise(keys[3], (POLES, FILTERS), (2.0 / (POLES * TOK_DEV * N_CTX) ** 0.5), 0.25, ((1, 8),), jnp.float32),
        "decay_rate": jnp.clip(jnp.exp(math.log(0.05) - 7.8477626 * jax.random.uniform(keys[4], (POLES, FILTERS), jnp.float32) ** level_of(keys[4], (POLES, FILTERS), ((1, 8),), -0.2, 0.2)), 1.9531249563442543e-05, 0.05),
        "skip_gain": noise(keys[5], (D,), 1.0, 4.0, ((0, 8),), jnp.float32),
        "cotangent": noise(keys[6], (N_DP, N_CTX, CAP, D), 1.0, 6.0, ((0, 4), (1, 8))),
    }


def causal(filt, signal):
    size = 2 * signal.shape[0]
    spec = jnp.fft.rfft(filt, n=size, axis=0) * jnp.fft.rfft(signal, n=size, axis=0)
    return jnp.fft.irfft(spec, n=size, axis=0)[: signal.shape[0]]


def correlate(later, earlier):
    size = 2 * later.shape[0]
    spec = jnp.fft.rfft(later, n=size, axis=0) * jnp.conj(jnp.fft.rfft(earlier, n=size, axis=0))
    return jnp.fft.irfft(spec, n=size, axis=0)[: later.shape[0]]


def reference(features, counts, short_taps, residue, decay_rate, skip_gain, cotangent):
    window_len = TOK_DEV * N_CTX
    positions = jnp.arange(window_len, dtype=jnp.int32)
    times = jnp.arange(window_len, dtype=jnp.float32)
    basis = jnp.exp(-decay_rate[:, None, :] * times[None, :, None])
    filt = jnp.sum(residue[:, None, :] * basis, axis=0)
    filt_chan = jnp.repeat(filt, GROUP, axis=1)
    slot_rows = jnp.arange(CAP, dtype=jnp.int32)

    def replica(inputs):
        feats_b, counts_b, cot_b = inputs
        shard_ends = jnp.cumsum(counts_b).astype(jnp.int32)
        shard_starts = (shard_ends - counts_b).astype(jnp.int32)
        passed = shard_ends[None, :] <= positions[:, None]
        shard_of = jnp.sum(passed.astype(jnp.int32), axis=1).astype(jnp.int32)
        before = jnp.sum(jnp.where(passed, counts_b[None, :], 0), axis=1).astype(jnp.int32)
        take_index = (shard_of * CAP + positions - before).astype(jnp.int32)
        window = feats_b.reshape(N_CTX * CAP, 3, D)[take_index]
        padded = jnp.pad(window, ((TAPS - 1, 0), (0, 0), (0, 0)))
        short_out = jnp.zeros((window_len, 3, D), jnp.float32)
        for tap_index in range(TAPS):
            piece = padded[TAPS - 1 - tap_index: TAPS - 1 - tap_index + window_len].astype(jnp.float32)
            short_out = short_out + short_taps[tap_index] * piece
        short_b = short_out.astype(jnp.bfloat16)
        query_f = short_b[:, 0].astype(jnp.float32)
        key_f = short_b[:, 1].astype(jnp.float32)
        value_f = short_b[:, 2].astype(jnp.float32)
        mixed = (key_f * value_f).astype(jnp.bfloat16).astype(jnp.float32)
        long_out = causal(filt_chan, mixed) + skip_gain * mixed
        gated = (query_f * long_out).astype(jnp.bfloat16)
        back_index = jnp.clip(shard_starts[:, None] + slot_rows[None, :], 0, window_len - 1).astype(jnp.int32)
        back_valid = slot_rows[None, :] < counts_b[:, None]
        out_rows = jnp.where(back_valid[:, :, None], gated[back_index], jnp.zeros((), jnp.bfloat16))
        grad_f = cot_b.reshape(N_CTX * CAP, D)[take_index].astype(jnp.float32)
        d_query = grad_f * long_out
        d_long = grad_f * query_f
        d_mixed = jnp.flip(causal(filt_chan, jnp.flip(d_long, axis=0)), axis=0) + skip_gain * d_long
        d_short = jnp.stack([d_query, d_mixed * value_f, d_mixed * key_f], axis=1)
        tail = jnp.pad(d_short, ((0, TAPS - 1), (0, 0), (0, 0)))
        d_window = jnp.zeros((window_len, 3, D), jnp.float32)
        tap_grads = []
        for tap_index in range(TAPS):
            d_window = d_window + short_taps[tap_index] * tail[tap_index: tap_index + window_len]
            piece = padded[TAPS - 1 - tap_index: TAPS - 1 - tap_index + window_len].astype(jnp.float32)
            tap_grads.append(jnp.sum(d_short * piece, axis=0))
        d_window = d_window.astype(jnp.bfloat16)
        d_rows = jnp.where(back_valid[:, :, None, None], d_window[back_index], jnp.zeros((), jnp.bfloat16))
        d_rows = d_rows.reshape(N_CTX, CAP, 3 * D)
        lag_grad = correlate(d_long, mixed).reshape(window_len, FILTERS, GROUP).sum(axis=2)
        d_res = jnp.sum(basis * lag_grad[None], axis=1)
        d_skip = jnp.sum(d_long * mixed, axis=0)
        return out_rows, d_rows, jnp.stack(tap_grads, axis=0), d_res, d_skip

    outs = lax.map(replica, (features, counts, cotangent))
    return outs[0], outs[1], jnp.sum(outs[2], axis=0), jnp.sum(outs[3], axis=0), jnp.sum(outs[4], axis=0)
```

```python
import functools

import jax
import jax.numpy as jnp
from jax import lax
from jax.experimental import pallas as pl
from jax.experimental.pallas import tpu as pltpu
from jax.sharding import PartitionSpec as P

TAPS = 7
HALO = 8
REACH = TAPS - 1
ROWS = 256
BLK = 128
POLES = 16
GROUP = 16
LANES = 128
PER = LANES // GROUP
F32 = jnp.float32
BF16 = jnp.bfloat16
SKIP_ROW = 3 * TAPS
RES_ROW = SKIP_ROW + 1
DEC_ROW = SKIP_ROW + 2
CNT_ROW = SKIP_ROW + 3
PARAM_ROWS = 32
GRAD_ROWS = 24


def iota(shape, axis):
    return lax.broadcasted_iota(jnp.int32, shape, axis)


def same_filter():
    return (iota((LANES, LANES), 0) // POLES) == (iota((LANES, LANES), 1) // GROUP)


def lane_filter(width):
    return (iota((1, width), 1) % LANES) // GROUP


def column_of(row):
    return jnp.transpose(jnp.broadcast_to(row, (LANES, LANES)))


def fold(full):
    return jnp.sum(full.reshape(PER, POLES, LANES), axis=0)


def unfold(compact):
    return jnp.where(same_filter(), jnp.tile(compact, (PER, 1)), 0.0)


def fill(scratch, rows_bf, left, right, count, capacity):
    own = rows_bf.astype(F32)
    keep = iota((capacity, LANES), 0) < count
    if left is None:
        scratch[0:HALO, :] = jnp.zeros((HALO, LANES), F32)
    else:
        scratch[0:HALO, :] = left.astype(F32)
    scratch[HALO : HALO + capacity, :] = jnp.where(keep, own, 0.0)
    tail_rows = scratch.shape[0] - HALO - capacity
    scratch[HALO + capacity :, :] = jnp.zeros((tail_rows, LANES), F32)
    scratch[pl.ds(HALO + count, HALO), :] = right.astype(F32)


def short_conv(scratch, taps_of):
    total = taps_of(0) * scratch[HALO : HALO + ROWS, :]
    for tap in range(1, TAPS):
        total = total + taps_of(tap) * scratch[HALO - tap : HALO - tap + ROWS, :]
    return total.astype(BF16).astype(F32)


def front(lanes, count, feats, cot, tail, head, cot_head, param, win, grad):
    capacity = cot.shape[0]
    shorts = []
    for m in range(3):
        fill(
            win.at[m], feats[m][:, lanes], tail[m][:, lanes], head[m][:, lanes], count, capacity
        )
        shorts.append(
            short_conv(win.at[m], lambda tap, m=m: param[0, pl.ds(3 * tap + m, 1), lanes])
        )
    fill(grad, cot[:, lanes], None, cot_head[:, lanes], count, capacity)
    query, key, value = shorts
    mixed = (key * value).astype(BF16).astype(F32)
    grad_rows = grad[HALO : HALO + ROWS, :]
    return query, key, value, mixed, grad_rows, grad_rows * query


def state_kernel(groups, sc, fq, fk, fv, cot, tq, tk, tv, hq, hk, hv, hc, param, out, win, grad):
    count = sc[0]

    def group(k, carry):
        lanes = pl.ds(pl.multiple_of(k * LANES, LANES), LANES)
        _, _, _, mixed, _, d_long = front(
            lanes, count, (fq, fk, fv), cot, (tq, tk, tv), (hq, hk, hv), hc, param, win, grad
        )
        dec = column_of(param[0, DEC_ROW : DEC_ROW + 1, lanes])
        dec = jnp.concatenate([dec, dec], axis=1)
        step = iota((LANES, ROWS), 1)
        ahead = count - 1 - step
        powers = jnp.where(ahead >= 0, jnp.exp(-dec * jnp.maximum(ahead, 0).astype(F32)), 0.0)
        after = step - REACH
        inside = jnp.logical_and(after >= 0, after < count)
        back = jnp.where(inside, jnp.exp(-dec * jnp.maximum(after, 0).astype(F32)), 0.0)
        fwd = jnp.dot(powers.astype(BF16), mixed.astype(BF16), preferred_element_type=F32)
        bwd = jnp.dot(back.astype(BF16), d_long.astype(BF16), preferred_element_type=F32)
        same = same_filter()
        out[0:POLES, lanes] = fold(jnp.where(same, fwd, 0.0)).astype(BF16)
        out[POLES : 2 * POLES, lanes] = fold(jnp.where(same, bwd, 0.0)).astype(BF16)
        return carry

    lax.fori_loop(0, groups, group, 0)


def main_kernel(
    groups, shards, sc, fq, fk, fv, cot, tq, tk, tv, hq, hk, hv, hc, param, states,
    out, dfeat, dparam, win, grad, dshort, dwin,
):
    count = sc[0]
    m_step = pl.program_id(1)
    capacity = cot.shape[0]

    def group(k, carry):
        lanes = pl.ds(pl.multiple_of(k * LANES, LANES), LANES)
        query, key, value, mixed, grad_rows, d_long = front(
            lanes, count, (fq, fk, fv), cot, (tq, tk, tv), (hq, hk, hv), hc, param, win, grad
        )
        row = iota((ROWS, LANES), 0)
        reach = row < count + REACH
        own = row < count
        mixed = jnp.where(reach, mixed, 0.0)
        d_long = jnp.where(reach, d_long, 0.0)
        d_own = jnp.where(own, d_long, 0.0)
        same = same_filter()
        res_row = param[0, RES_ROW : RES_ROW + 1, lanes]
        dec_row = param[0, DEC_ROW : DEC_ROW + 1, lanes]
        skip = param[0, SKIP_ROW : SKIP_ROW + 1, lanes]
        res = column_of(res_row)
        dec = column_of(dec_row)
        lane_f = iota((LANES, LANES), 1).astype(F32)
        sub_f = iota((LANES, LANES), 0).astype(F32)

        rate = fold(jnp.where(same, dec, 0.0))
        from_left = jnp.zeros((POLES, LANES), F32)
        from_right = jnp.zeros((POLES, LANES), F32)
        for i in range(shards):
            gap_l = sc[1 + i]
            gap_r = sc[1 + shards + i]
            w_l = jnp.where(gap_l >= 0, jnp.exp(-rate * jnp.maximum(gap_l, 0).astype(F32)), 0.0)
            w_r = jnp.where(gap_r >= 0, jnp.exp(-rate * jnp.maximum(gap_r, 0).astype(F32)), 0.0)
            both = states[i, :, lanes].astype(F32)
            from_left = from_left + w_l * both[0:POLES]
            from_right = from_right + w_r * both[POLES : 2 * POLES]

        pw_lag = jnp.exp(-dec * lane_f)
        turned = (iota((LANES, LANES), 1) * (LANES - 1)) % LANES
        pw_turn = jnp.exp(-dec * turned.astype(F32))
        k_lag = jnp.sum((res * pw_lag).reshape(PER, POLES, LANES), axis=1)
        k_turn = jnp.sum((res * pw_turn).reshape(PER, POLES, LANES), axis=1)
        lower = iota((BLK, BLK), 0) >= iota((BLK, BLK), 1)
        upper = iota((BLK, BLK), 0) <= iota((BLK, BLK), 1)

        def toeplitz(rows, keep):
            parts = []
            for f in range(PER):
                wide = jnp.broadcast_to(rows[f : f + 1, :], (BLK, LANES))
                wide = pltpu.roll(wide, 0, 1, stride=1, stride_axis=0)
                parts.append(jnp.where(keep, wide, 0.0).astype(BF16))
            return jnp.concatenate(parts, axis=1)

        t_fwd = toeplitz(k_turn, lower)
        t_bwd = toeplitz(k_lag, upper)

        def side(x):
            return jnp.concatenate([x[0:BLK], x[BLK:ROWS]], axis=1)

        def stacked(x):
            fil = lane_filter(2 * LANES)
            return jnp.concatenate(
                [jnp.where(fil == f, x, 0.0).astype(BF16) for f in range(PER)], axis=0
            )

        m_side = side(mixed)
        d_side = side(d_long)
        own_side = side(d_own).astype(BF16)
        mirror = iota((BLK, BLK), 0) + iota((BLK, BLK), 1)
        flip = jnp.where(mirror == BLK - 1, 1.0, 0.0).astype(BF16)
        own_flip = jnp.dot(flip, own_side, preferred_element_type=F32).astype(BF16)
        m_stack = stacked(m_side)
        d_stack = stacked(d_side)
        y_fwd = jnp.dot(t_fwd, m_stack, preferred_element_type=F32)
        y_bwd = jnp.dot(t_bwd, d_stack, preferred_element_type=F32)
        pair = lax.dot_general(
            own_flip, m_stack, (((1,), (1,)), ((), ())), preferred_element_type=F32
        )

        pw_rest = jnp.exp(-dec * (BLK - 1.0 - lane_f))
        in_pw = pw_rest.astype(BF16)
        out_pw = jnp.exp(-dec * (lane_f + 1.0)).astype(BF16)
        s_first = jnp.dot(in_pw, mixed[0:BLK].astype(BF16), preferred_element_type=F32)
        carry0 = unfold(from_left)
        carry1 = jnp.exp(-dec * float(BLK)) * carry0 + jnp.where(same, s_first, 0.0)
        carries = jnp.concatenate([carry0, carry1], axis=1)
        out_t = (res_row * jnp.exp(-dec_row * (sub_f + 1.0))).astype(BF16)
        y_fwd = y_fwd + jnp.dot(out_t, carries.astype(BF16), preferred_element_type=F32)
        seen = jnp.dot(out_pw, own_side, preferred_element_type=F32)

        e_second = jnp.dot(out_pw, d_long[BLK:ROWS].astype(BF16), preferred_element_type=F32)
        e_second = jnp.where(same, e_second, 0.0).astype(BF16)
        in_t = (res_row * jnp.exp(-dec_row * (BLK - 1.0 - sub_f))).astype(BF16)
        until = jnp.maximum(count + REACH - row, 0).astype(F32)
        far_t = (res_row * jnp.exp(-dec_row * until)).astype(BF16)
        y_far = jnp.dot(far_t, unfold(from_right).astype(BF16), preferred_element_type=F32)
        y_near = jnp.dot(in_t, e_second, preferred_element_type=F32)

        long_out = jnp.concatenate([y_fwd[:, 0:LANES], y_fwd[:, LANES:]], axis=0) + skip * mixed
        d_mixed = (
            jnp.concatenate([y_bwd[:, 0:LANES] + y_near, y_bwd[:, LANES:]], axis=0)
            + y_far
            + skip * d_long
        )
        gated = jnp.where(own, query * long_out, 0.0)
        out[:, lanes] = gated[0:capacity].astype(BF16)

        lag_rows = []
        for f in range(PER):
            piece = jnp.where(mirror < BLK, pair[:, f * LANES : (f + 1) * LANES], 0.0)
            piece = pltpu.roll(piece, 0, 1, stride=1, stride_axis=0)
            lag_rows.append(jnp.broadcast_to(jnp.sum(piece, axis=0, keepdims=True), (POLES, LANES)))
        lag_sums = jnp.concatenate(lag_rows, axis=0)
        crossed = seen * carries
        res_grad = lag_sums * pw_rest + crossed[:, 0:LANES] + crossed[:, LANES:]
        dparam[RES_ROW : RES_ROW + 1, lanes] = jnp.sum(
            jnp.transpose(res_grad), axis=0, keepdims=True
        )
        dparam[SKIP_ROW : SKIP_ROW + 1, lanes] = jnp.sum(d_own * mixed, axis=0, keepdims=True)

        d_parts = (grad_rows * long_out, d_mixed * value, d_mixed * key)
        for m in range(3):
            d_m = jnp.where(reach, d_parts[m], 0.0)
            dshort[0:ROWS, :] = d_m
            d_m = jnp.where(own, d_m, 0.0)
            total = jnp.zeros((capacity, LANES), F32)
            for tap in range(TAPS):
                weight = param[0, 3 * tap + m : 3 * tap + m + 1, lanes]
                total = total + weight * dshort[tap : tap + capacity, :]
                piece = d_m * win[m, HALO - tap : HALO - tap + ROWS, :]
                dparam[3 * tap + m : 3 * tap + m + 1, lanes] = jnp.sum(
                    piece, axis=0, keepdims=True
                )
            dwin[m, :, lanes] = jnp.where(own[0:capacity], total, 0.0).astype(BF16)
        return carry

    @pl.when(m_step == 0)
    def _():
        dparam[GRAD_ROWS - 1 : GRAD_ROWS, :] = jnp.zeros((1, dparam.shape[1]), F32)
        dshort[ROWS:, :] = jnp.zeros((dshort.shape[0] - ROWS, LANES), F32)
        lax.fori_loop(0, groups, group, 0)

    dfeat[...] = dwin[m_step]


def per_device(features, counts, short_taps, residue, decay_rate, skip_gain, cotangent):
    shards = lax.axis_size("ctx")
    me = lax.axis_index("ctx")
    capacity = features.shape[2]
    width = cotangent.shape[3]
    chan = short_taps.shape[2]
    groups = chan // LANES
    feats = features[0, 0]
    cot = cotangent[0, 0]
    count = counts[0, 0]

    packed = jnp.concatenate(
        [
            short_taps.reshape(3 * TAPS, chan),
            skip_gain.reshape(1, chan),
            residue.T.reshape(1, chan),
            decay_rate.T.reshape(1, chan),
            jnp.broadcast_to(count.astype(F32), (PARAM_ROWS - CNT_ROW, chan)),
        ],
        axis=0,
    )
    params = lax.all_gather(packed, "ctx", axis=0, tiled=False)
    tail = lax.dynamic_slice(feats, (count - HALO, 0), (HALO, 3 * width))
    head = jnp.concatenate([feats[0:HALO], cot[0:HALO]], axis=1)
    tail = lax.ppermute(tail, "ctx", [(i, i + 1) for i in range(shards - 1)])
    head = lax.ppermute(head, "ctx", [(i + 1, i) for i in range(shards - 1)])

    all_counts = params[:, CNT_ROW, 0].astype(jnp.int32)
    ends = jnp.cumsum(all_counts)
    starts = ends - all_counts
    ids = jnp.arange(shards, dtype=jnp.int32)
    gap_l = jnp.where(ids < me, starts[me] - ends, -1)
    gap_r = jnp.where(ids > me, starts - ends[me], -1)
    scalars = jnp.concatenate([count[None], gap_l, gap_r]).astype(jnp.int32)

    def cols(rows, offset):
        return pl.BlockSpec((rows, chan), lambda g, *_: (0, offset * shards + g))

    smem = pl.BlockSpec(memory_space=pltpu.SMEM)
    specs = [smem]
    specs += [cols(capacity, m) for m in range(3)] + [cols(capacity, 0)]
    specs += [cols(HALO, m) for m in range(3)] + [cols(HALO, m) for m in range(4)]
    specs += [pl.BlockSpec((1, PARAM_ROWS, chan), lambda g, *_: (g, 0, 0))]
    args = [scalars, feats, feats, feats, cot, tail, tail, tail, head, head, head, head, params]
    ext = HALO + ROWS + HALO
    states = pl.pallas_call(
        functools.partial(state_kernel, groups),
        grid=(shards,),
        in_specs=specs,
        out_specs=cols(2 * POLES, 0),
        out_shape=jax.ShapeDtypeStruct((2 * POLES, width), BF16),
        scratch_shapes=[pltpu.VMEM((3, ext, LANES), F32), pltpu.VMEM((ext, LANES), F32)],
        name="states",
    )(*args)
    states = lax.all_gather(states, "ctx", axis=0, tiled=False)

    out, dfeat, dparam = pl.pallas_call(
        functools.partial(main_kernel, groups, shards),
        grid=(shards, 3),
        in_specs=specs + [pl.BlockSpec((shards, 2 * POLES, chan), lambda g, *_: (0, 0, g))],
        out_specs=[
            cols(capacity, 0),
            pl.BlockSpec((capacity, chan), lambda g, m: (0, m * shards + g)),
            cols(GRAD_ROWS, 0),
        ],
        out_shape=[
            jax.ShapeDtypeStruct((capacity, width), BF16),
            jax.ShapeDtypeStruct((capacity, 3 * width), BF16),
            jax.ShapeDtypeStruct((GRAD_ROWS, width), F32),
        ],
        scratch_shapes=[
            pltpu.VMEM((3, ext, LANES), F32),
            pltpu.VMEM((ext, LANES), F32),
            pltpu.VMEM((ROWS + HALO, LANES), F32),
            pltpu.VMEM((3, capacity, chan), BF16),
        ],
        name="main",
    )(*args, states)
    grads = lax.psum_scatter(dparam, "ctx", scatter_dimension=1, tiled=True)
    grads = lax.psum(grads, "dp")
    return (
        out[None, None],
        dfeat[None, None],
        grads[0 : 3 * TAPS].reshape(TAPS, 3, chan),
        grads[RES_ROW].reshape(chan // GROUP, POLES).T,
        grads[SKIP_ROW],
    )


def solution(mesh):
    in_specs = (
        P("dp", "ctx", None, None),
        P("dp", "ctx"),
        P(None, None, "ctx"),
        P(None, "ctx"),
        P(None, "ctx"),
        P("ctx"),
        P("dp", "ctx", None, None),
    )
    out_specs = (
        P("dp", "ctx", None, None),
        P("dp", "ctx", None, None),
        P(None, None, "ctx"),
        P(None, "ctx"),
        P("ctx"),
    )
    return jax.shard_map(
        per_device, mesh=mesh, in_specs=in_specs, out_specs=out_specs, check_vma=False
    )
```

```python
import functools

import jax
import jax.numpy as jnp
from jax import lax
from jax.experimental import pallas as pl
from jax.experimental.pallas import tpu as pltpu
from jax.sharding import PartitionSpec as P

TAPS = 7
HALO = 8
REACH = TAPS - 1
ROWS = 256
BLK = 128
POLES = 16
GROUP = 16
LANES = 128
PER = LANES // GROUP
F32 = jnp.float32
BF16 = jnp.bfloat16
SKIP_ROW = 3 * TAPS
RES_ROW = SKIP_ROW + 1
DEC_ROW = SKIP_ROW + 2
CNT_ROW = SKIP_ROW + 3
PARAM_ROWS = 32
GRAD_ROWS = 24


def iota(shape, axis):
    return lax.broadcasted_iota(jnp.int32, shape, axis)


def same_filter():
    return (iota((LANES, LANES), 0) // POLES) == (iota((LANES, LANES), 1) // GROUP)


def lane_filter(width):
    return (iota((1, width), 1) % LANES) // GROUP


def column_of(row):
    return jnp.transpose(jnp.broadcast_to(row, (LANES, LANES)))


def fold(full):
    return jnp.sum(full.reshape(PER, POLES, LANES), axis=0)


def unfold(compact):
    return jnp.where(same_filter(), jnp.tile(compact, (PER, 1)), 0.0)


def fill(scratch, rows_bf, left, right, sc, capacity):
    count = sc[0]
    own = rows_bf.astype(F32)
    keep = iota((capacity, LANES), 0) < count
    if left is None:
        scratch[0:HALO, :] = jnp.zeros((HALO, LANES), F32)
    else:
        scratch[0:HALO, :] = jnp.where(sc[1] > 0, left.astype(F32), 0.0)
    scratch[HALO : HALO + capacity, :] = jnp.where(keep, own, 0.0)
    tail_rows = scratch.shape[0] - HALO - capacity
    scratch[HALO + capacity :, :] = jnp.zeros((tail_rows, LANES), F32)
    scratch[pl.ds(HALO + count, HALO), :] = jnp.where(sc[2] > 0, right.astype(F32), 0.0)


def short_conv(scratch, taps_of):
    total = taps_of(0) * scratch[HALO : HALO + ROWS, :]
    for tap in range(1, TAPS):
        total = total + taps_of(tap) * scratch[HALO - tap : HALO - tap + ROWS, :]
    return total.astype(BF16).astype(F32)


def front(lanes, sc, feats, cot, tail, head, cot_head, param, win, grad):
    capacity = cot.shape[0]
    shorts = []
    for m in range(3):
        fill(
            win.at[m], feats[m][:, lanes], tail[m][:, lanes], head[m][:, lanes], sc, capacity
        )
        shorts.append(
            short_conv(win.at[m], lambda tap, m=m: param[0, pl.ds(3 * tap + m, 1), lanes])
        )
    fill(grad, cot[:, lanes], None, cot_head[:, lanes], sc, capacity)
    query, key, value = shorts
    mixed = (key * value).astype(BF16).astype(F32)
    grad_rows = grad[HALO : HALO + ROWS, :]
    return query, key, value, mixed, grad_rows, grad_rows * query


def state_kernel(groups, sc, fq, fk, fv, cot, tq, tk, tv, hq, hk, hv, hc, param, out, win, grad):
    count = sc[0]

    def group(k, carry):
        lanes = pl.ds(pl.multiple_of(k * LANES, LANES), LANES)
        _, _, _, mixed, _, d_long = front(
            lanes, sc, (fq, fk, fv), cot, (tq, tk, tv), (hq, hk, hv), hc, param, win, grad
        )
        dec = column_of(param[0, DEC_ROW : DEC_ROW + 1, lanes])
        dec = jnp.concatenate([dec, dec], axis=1)
        step = iota((LANES, ROWS), 1)
        ahead = count - 1 - step
        powers = jnp.where(ahead >= 0, jnp.exp(-dec * jnp.maximum(ahead, 0).astype(F32)), 0.0)
        after = step - REACH
        inside = jnp.logical_and(after >= 0, after < count)
        back = jnp.where(inside, jnp.exp(-dec * jnp.maximum(after, 0).astype(F32)), 0.0)
        fwd = jnp.dot(powers.astype(BF16), mixed.astype(BF16), preferred_element_type=F32)
        bwd = jnp.dot(back.astype(BF16), d_long.astype(BF16), preferred_element_type=F32)
        same = same_filter()
        out[0, :, lanes] = fold(jnp.where(same, fwd, 0.0)).astype(BF16)
        out[1, :, lanes] = fold(jnp.where(same, bwd, 0.0)).astype(BF16)
        return carry

    lax.fori_loop(0, groups, group, 0)


def main_kernel(
    groups, shards, sc, fq, fk, fv, cot, tq, tk, tv, hq, hk, hv, hc, param, states,
    out, dfeat, dparam, win, grad, dshort, dwin,
):
    count = sc[0]
    m_step = pl.program_id(1)
    capacity = cot.shape[0]

    def group(k, carry):
        lanes = pl.ds(pl.multiple_of(k * LANES, LANES), LANES)
        query, key, value, mixed, grad_rows, d_long = front(
            lanes, sc, (fq, fk, fv), cot, (tq, tk, tv), (hq, hk, hv), hc, param, win, grad
        )
        row = iota((ROWS, LANES), 0)
        reach = row < count + REACH
        own = row < count
        mixed = jnp.where(reach, mixed, 0.0)
        d_long = jnp.where(reach, d_long, 0.0)
        d_own = jnp.where(own, d_long, 0.0)
        same = same_filter()
        res_row = param[0, RES_ROW : RES_ROW + 1, lanes]
        dec_row = param[0, DEC_ROW : DEC_ROW + 1, lanes]
        skip = param[0, SKIP_ROW : SKIP_ROW + 1, lanes]
        res = column_of(res_row)
        dec = column_of(dec_row)
        lane_f = iota((LANES, LANES), 1).astype(F32)
        sub_f = iota((LANES, LANES), 0).astype(F32)

        rate = fold(jnp.where(same, dec, 0.0))
        from_left = jnp.zeros((POLES, LANES), F32)
        from_right = jnp.zeros((POLES, LANES), F32)
        for i in range(shards):
            gap_l = sc[3 + i]
            gap_r = sc[3 + shards + i]
            gap = jnp.maximum(gap_l, gap_r)
            there = states[i, :, lanes].astype(F32)
            there = there * jnp.exp(-rate * jnp.maximum(gap, 0).astype(F32))
            from_left = from_left + jnp.where(gap_l >= 0, there, 0.0)
            from_right = from_right + jnp.where(gap_r >= 0, there, 0.0)

        pw_lag = jnp.exp(-dec * lane_f)
        turned = (iota((LANES, LANES), 1) * (LANES - 1)) % LANES
        pw_turn = jnp.exp(-dec * turned.astype(F32))
        k_lag = jnp.sum((res * pw_lag).reshape(PER, POLES, LANES), axis=1)
        k_turn = jnp.sum((res * pw_turn).reshape(PER, POLES, LANES), axis=1)
        lower = iota((BLK, BLK), 0) >= iota((BLK, BLK), 1)
        upper = iota((BLK, BLK), 0) <= iota((BLK, BLK), 1)

        def toeplitz(rows, keep):
            parts = []
            for f in range(PER):
                wide = jnp.broadcast_to(rows[f : f + 1, :], (BLK, LANES))
                wide = pltpu.roll(wide, 0, 1, stride=1, stride_axis=0)
                parts.append(jnp.where(keep, wide, 0.0).astype(BF16))
            return jnp.concatenate(parts, axis=1)

        t_fwd = toeplitz(k_turn, lower)
        t_bwd = toeplitz(k_lag, upper)

        def side(x):
            return jnp.concatenate([x[0:BLK], x[BLK:ROWS]], axis=1)

        def stacked(x):
            fil = lane_filter(2 * LANES)
            return jnp.concatenate(
                [jnp.where(fil == f, x, 0.0).astype(BF16) for f in range(PER)], axis=0
            )

        m_side = side(mixed)
        d_side = side(d_long)
        own_side = side(d_own).astype(BF16)
        mirror = iota((BLK, BLK), 0) + iota((BLK, BLK), 1)
        flip = jnp.where(mirror == BLK - 1, 1.0, 0.0).astype(BF16)
        own_flip = jnp.dot(flip, own_side, preferred_element_type=F32).astype(BF16)
        m_stack = stacked(m_side)
        d_stack = stacked(d_side)
        y_fwd = jnp.dot(t_fwd, m_stack, preferred_element_type=F32)
        y_bwd = jnp.dot(t_bwd, d_stack, preferred_element_type=F32)
        pair = lax.dot_general(
            own_flip, m_stack, (((1,), (1,)), ((), ())), preferred_element_type=F32
        )

        pw_rest = jnp.exp(-dec * (BLK - 1.0 - lane_f))
        in_pw = pw_rest.astype(BF16)
        out_pw = jnp.exp(-dec * (lane_f + 1.0)).astype(BF16)
        s_first = jnp.dot(in_pw, mixed[0:BLK].astype(BF16), preferred_element_type=F32)
        carry0 = unfold(from_left)
        carry1 = jnp.exp(-dec * float(BLK)) * carry0 + jnp.where(same, s_first, 0.0)
        carries = jnp.concatenate([carry0, carry1], axis=1)
        out_t = (res_row * jnp.exp(-dec_row * (sub_f + 1.0))).astype(BF16)
        y_fwd = y_fwd + jnp.dot(out_t, carries.astype(BF16), preferred_element_type=F32)
        seen = jnp.dot(out_pw, own_side, preferred_element_type=F32)

        e_second = jnp.dot(out_pw, d_long[BLK:ROWS].astype(BF16), preferred_element_type=F32)
        e_second = jnp.where(same, e_second, 0.0).astype(BF16)
        in_t = (res_row * jnp.exp(-dec_row * (BLK - 1.0 - sub_f))).astype(BF16)
        until = jnp.maximum(count + REACH - row, 0).astype(F32)
        far_t = (res_row * jnp.exp(-dec_row * until)).astype(BF16)
        y_far = jnp.dot(far_t, unfold(from_right).astype(BF16), preferred_element_type=F32)
        y_near = jnp.dot(in_t, e_second, preferred_element_type=F32)

        long_out = jnp.concatenate([y_fwd[:, 0:LANES], y_fwd[:, LANES:]], axis=0) + skip * mixed
        d_mixed = (
            jnp.concatenate([y_bwd[:, 0:LANES] + y_near, y_bwd[:, LANES:]], axis=0)
            + y_far
            + skip * d_long
        )
        gated = jnp.where(own, query * long_out, 0.0)
        out[:, lanes] = gated[0:capacity].astype(BF16)

        lag_rows = []
        for f in range(PER):
            piece = jnp.where(mirror < BLK, pair[:, f * LANES : (f + 1) * LANES], 0.0)
            piece = pltpu.roll(piece, 0, 1, stride=1, stride_axis=0)
            lag_rows.append(jnp.broadcast_to(jnp.sum(piece, axis=0, keepdims=True), (POLES, LANES)))
        lag_sums = jnp.concatenate(lag_rows, axis=0)
        crossed = seen * carries
        res_grad = lag_sums * pw_rest + crossed[:, 0:LANES] + crossed[:, LANES:]
        dparam[RES_ROW : RES_ROW + 1, lanes] = jnp.sum(
            jnp.transpose(res_grad), axis=0, keepdims=True
        )
        dparam[SKIP_ROW : SKIP_ROW + 1, lanes] = jnp.sum(d_own * mixed, axis=0, keepdims=True)

        d_parts = (grad_rows * long_out, d_mixed * value, d_mixed * key)
        for m in range(3):
            d_m = jnp.where(reach, d_parts[m], 0.0)
            dshort[0:ROWS, :] = d_m
            d_m = jnp.where(own, d_m, 0.0)
            total = jnp.zeros((capacity, LANES), F32)
            for tap in range(TAPS):
                weight = param[0, 3 * tap + m : 3 * tap + m + 1, lanes]
                total = total + weight * dshort[tap : tap + capacity, :]
                piece = d_m * win[m, HALO - tap : HALO - tap + ROWS, :]
                dparam[3 * tap + m : 3 * tap + m + 1, lanes] = jnp.sum(
                    piece, axis=0, keepdims=True
                )
            dwin[m, :, lanes] = jnp.where(own[0:capacity], total, 0.0).astype(BF16)
        return carry

    @pl.when(m_step == 0)
    def _():
        dparam[GRAD_ROWS - 1 : GRAD_ROWS, :] = jnp.zeros((1, dparam.shape[1]), F32)
        dshort[ROWS:, :] = jnp.zeros((dshort.shape[0] - ROWS, LANES), F32)
        lax.fori_loop(0, groups, group, 0)

    dfeat[...] = dwin[m_step]


MESH = pl.DeviceIdType.MESH


def meet(peers):
    barrier = pltpu.get_barrier_semaphore()
    for peer in peers:
        pl.semaphore_signal(barrier, inc=1, device_id=peer, device_id_type=MESH)
    pl.semaphore_wait(barrier, len(peers))


def params_kernel(shards, packed, tail, head, params, tail_in, head_in, send, recv, own):
    dp, me = lax.axis_index("dp"), lax.axis_index("ctx")
    peers = [(dp, lax.rem(me + d, shards)) for d in range(1, shards)]
    meet(peers)
    local = pltpu.make_async_copy(packed, params.at[me], own)
    local.start()
    jobs = [(tail, tail_in, peers[0]), (head, head_in, peers[-1])]
    jobs += [(packed, params.at[me], peer) for peer in peers]
    copies = []
    for n, (src, dst, peer) in enumerate(jobs):
        copies.append(
            pltpu.make_async_remote_copy(
                src_ref=src, dst_ref=dst, send_sem=send.at[n], recv_sem=recv.at[n],
                device_id=peer, device_id_type=MESH,
            )
        )
        copies[-1].start()
    local.wait()
    for copy in copies:
        copy.wait()


def spread_kernel(shards, states, seen, send, recv):
    dp, me = lax.axis_index("dp"), lax.axis_index("ctx")
    peers = [(dp, lax.rem(me + d, shards)) for d in range(1, shards)]
    meet(peers)
    copies = []
    for n, peer in enumerate(peers):
        way = (peer[1] < me).astype(jnp.int32)
        copies.append(
            pltpu.make_async_remote_copy(
                src_ref=states.at[way], dst_ref=seen.at[me], send_sem=send.at[n],
                recv_sem=recv.at[n], device_id=peer, device_id_type=MESH,
            )
        )
        copies[-1].start()
    for copy in copies:
        copy.wait()


def reduce_kernel(shards, replicas, part, out, by_ctx, by_dp, send, recv, send_dp, recv_dp):
    dp, me = lax.axis_index("dp"), lax.axis_index("ctx")
    chan = out.shape[1]
    peers = [(dp, lax.rem(me + d, shards)) for d in range(1, shards)]
    others = [(lax.rem(dp + d, replicas), me) for d in range(1, replicas)]
    meet(peers + others)
    copies = []
    for n, peer in enumerate(peers):
        lanes = pl.ds(pl.multiple_of(peer[1] * chan, LANES), chan)
        copies.append(
            pltpu.make_async_remote_copy(
                src_ref=part.at[:, lanes], dst_ref=by_ctx.at[n], send_sem=send.at[n],
                recv_sem=recv.at[n], device_id=peer, device_id_type=MESH,
            )
        )
        copies[-1].start()
    total = part[:, pl.ds(pl.multiple_of(me * chan, LANES), chan)]
    for n, copy in enumerate(copies):
        copy.wait()
        total = total + by_ctx[n]
    by_dp[dp] = total
    copies = []
    for n, peer in enumerate(others):
        copies.append(
            pltpu.make_async_remote_copy(
                src_ref=by_dp.at[dp], dst_ref=by_dp.at[dp], send_sem=send_dp.at[n],
                recv_sem=recv_dp.at[n], device_id=peer, device_id_type=MESH,
            )
        )
        copies[-1].start()
    for copy in copies:
        copy.wait()
    total = by_dp[0]
    for n in range(1, replicas):
        total = total + by_dp[n]
    out[...] = total


def remote(ident):
    return pltpu.CompilerParams(collective_id=ident, has_side_effects=True)


def per_device(features, counts, short_taps, residue, decay_rate, skip_gain, cotangent):
    shards = lax.axis_size("ctx")
    me = lax.axis_index("ctx")
    capacity = features.shape[2]
    width = cotangent.shape[3]
    chan = short_taps.shape[2]
    groups = chan // LANES
    feats = features[0, 0]
    cot = cotangent[0, 0]
    count = counts[0, 0]

    packed = jnp.concatenate(
        [
            short_taps.reshape(3 * TAPS, chan),
            skip_gain.reshape(1, chan),
            residue.T.reshape(1, chan),
            decay_rate.T.reshape(1, chan),
            jnp.broadcast_to(count.astype(F32), (PARAM_ROWS - CNT_ROW, chan)),
        ],
        axis=0,
    )
    tail = lax.dynamic_slice(feats, (count - HALO, 0), (HALO, 3 * width))
    head = jnp.concatenate([feats[0:HALO], cot[0:HALO]], axis=1)
    anywhere = pl.BlockSpec(memory_space=pl.ANY)
    params, tail, head = pl.pallas_call(
        functools.partial(params_kernel, shards),
        in_specs=[anywhere] * 3,
        out_specs=[anywhere] * 3,
        out_shape=[
            jax.ShapeDtypeStruct((shards,) + packed.shape, F32),
            jax.ShapeDtypeStruct(tail.shape, BF16),
            jax.ShapeDtypeStruct(head.shape, BF16),
        ],
        scratch_shapes=[
            pltpu.SemaphoreType.DMA((shards + 1,)),
            pltpu.SemaphoreType.DMA((shards + 1,)),
            pltpu.SemaphoreType.DMA,
        ],
        compiler_params=remote(0),
        name="params",
    )(packed, tail, head)

    all_counts = params[:, CNT_ROW, 0].astype(jnp.int32)
    ends = jnp.cumsum(all_counts)
    starts = ends - all_counts
    ids = jnp.arange(shards, dtype=jnp.int32)
    gap_l = jnp.where(ids < me, starts[me] - ends, -1)
    gap_r = jnp.where(ids > me, starts - ends[me], -1)
    edges = jnp.stack([me > 0, me < shards - 1]).astype(jnp.int32)
    scalars = jnp.concatenate([count[None], edges, gap_l, gap_r]).astype(jnp.int32)

    def cols(rows, offset):
        return pl.BlockSpec((rows, chan), lambda g, *_: (0, offset * shards + g))

    smem = pl.BlockSpec(memory_space=pltpu.SMEM)
    specs = [smem]
    specs += [cols(capacity, m) for m in range(3)] + [cols(capacity, 0)]
    specs += [cols(HALO, m) for m in range(3)] + [cols(HALO, m) for m in range(4)]
    specs += [pl.BlockSpec((1, PARAM_ROWS, chan), lambda g, *_: (g, 0, 0))]
    args = [scalars, feats, feats, feats, cot, tail, tail, tail, head, head, head, head, params]
    ext = HALO + ROWS + HALO
    states = pl.pallas_call(
        functools.partial(state_kernel, groups),
        grid=(shards,),
        in_specs=specs,
        out_specs=pl.BlockSpec((2, POLES, chan), lambda g: (0, 0, g)),
        out_shape=jax.ShapeDtypeStruct((2, POLES, width), BF16),
        scratch_shapes=[pltpu.VMEM((3, ext, LANES), F32), pltpu.VMEM((ext, LANES), F32)],
        name="states",
    )(*args)
    states = pl.pallas_call(
        functools.partial(spread_kernel, shards),
        in_specs=[anywhere],
        out_specs=anywhere,
        out_shape=jax.ShapeDtypeStruct((shards, POLES, width), BF16),
        scratch_shapes=[
            pltpu.SemaphoreType.DMA((shards - 1,)),
            pltpu.SemaphoreType.DMA((shards - 1,)),
        ],
        compiler_params=remote(1),
        name="spread",
    )(states)

    out, dfeat, dparam = pl.pallas_call(
        functools.partial(main_kernel, groups, shards),
        grid=(shards, 3),
        in_specs=specs + [pl.BlockSpec((shards, POLES, chan), lambda g, *_: (0, 0, g))],
        out_specs=[
            cols(capacity, 0),
            pl.BlockSpec((capacity, chan), lambda g, m: (0, m * shards + g)),
            cols(GRAD_ROWS, 0),
        ],
        out_shape=[
            jax.ShapeDtypeStruct((capacity, width), BF16),
            jax.ShapeDtypeStruct((capacity, 3 * width), BF16),
            jax.ShapeDtypeStruct((GRAD_ROWS, width), F32),
        ],
        scratch_shapes=[
            pltpu.VMEM((3, ext, LANES), F32),
            pltpu.VMEM((ext, LANES), F32),
            pltpu.VMEM((ROWS + HALO, LANES), F32),
            pltpu.VMEM((3, capacity, chan), BF16),
        ],
        name="main",
    )(*args, states)
    replicas = lax.axis_size("dp")
    vmem = pl.BlockSpec(memory_space=pltpu.VMEM)
    grads = pl.pallas_call(
        functools.partial(reduce_kernel, shards, replicas),
        in_specs=[vmem],
        out_specs=vmem,
        out_shape=jax.ShapeDtypeStruct((GRAD_ROWS, chan), F32),
        scratch_shapes=[
            pltpu.VMEM((shards - 1, GRAD_ROWS, chan), F32),
            pltpu.VMEM((replicas, GRAD_ROWS, chan), F32),
            pltpu.SemaphoreType.DMA((shards - 1,)),
            pltpu.SemaphoreType.DMA((shards - 1,)),
            pltpu.SemaphoreType.DMA((replicas - 1,)),
            pltpu.SemaphoreType.DMA((replicas - 1,)),
        ],
        compiler_params=remote(2),
        name="reduce",
    )(dparam)
    return (
        out[None, None],
        dfeat[None, None],
        grads[0 : 3 * TAPS].reshape(TAPS, 3, chan),
        grads[RES_ROW].reshape(chan // GROUP, POLES).T,
        grads[SKIP_ROW],
    )


def solution(mesh):
    in_specs = (
        P("dp", "ctx", None, None),
        P("dp", "ctx"),
        P(None, None, "ctx"),
        P(None, "ctx"),
        P(None, "ctx"),
        P("ctx"),
        P("dp", "ctx", None, None),
    )
    out_specs = (
        P("dp", "ctx", None, None),
        P("dp", "ctx", None, None),
        P(None, None, "ctx"),
        P(None, "ctx"),
        P("ctx"),
    )
    return jax.shard_map(
        per_device, mesh=mesh, in_specs=in_specs, out_specs=out_specs, check_vma=False
    )
```

```python
import functools

import jax
import jax.numpy as jnp
from jax import lax
from jax.experimental import pallas as pl
from jax.experimental.pallas import tpu as pltpu
from jax.sharding import PartitionSpec as P

TAPS = 7
HALO = 8
REACH = TAPS - 1
ROWS = 256
BLK = 128
POLES = 16
GROUP = 16
LANES = 128
PER = LANES // GROUP
F32 = jnp.float32
BF16 = jnp.bfloat16
SKIP_ROW = 3 * TAPS
RES_ROW = SKIP_ROW + 1
DEC_ROW = SKIP_ROW + 2
CNT_ROW = SKIP_ROW + 3
PARAM_ROWS = 32
GRAD_ROWS = 24


def iota(shape, axis):
    return lax.broadcasted_iota(jnp.int32, shape, axis)


def same_filter():
    return (iota((LANES, LANES), 0) // POLES) == (iota((LANES, LANES), 1) // GROUP)


def lane_filter(width):
    return (iota((1, width), 1) % LANES) // GROUP


def column_of(row):
    return jnp.transpose(jnp.broadcast_to(row, (LANES, LANES)))


def fold(full):
    return jnp.sum(full.reshape(PER, POLES, LANES), axis=0)


def unfold(compact):
    return jnp.where(same_filter(), jnp.tile(compact, (PER, 1)), 0.0)


def fill(scratch, rows_bf, left, right, sc, capacity):
    count = sc[0]
    own = rows_bf.astype(F32)
    keep = iota((capacity, LANES), 0) < count
    if left is None:
        scratch[0:HALO, :] = jnp.zeros((HALO, LANES), F32)
    else:
        scratch[0:HALO, :] = jnp.where(sc[1] > 0, left.astype(F32), 0.0)
    scratch[HALO : HALO + capacity, :] = jnp.where(keep, own, 0.0)
    tail_rows = scratch.shape[0] - HALO - capacity
    scratch[HALO + capacity :, :] = jnp.zeros((tail_rows, LANES), F32)
    scratch[pl.ds(HALO + count, HALO), :] = jnp.where(sc[2] > 0, right.astype(F32), 0.0)


def short_conv(scratch, taps_of):
    total = taps_of(0) * scratch[HALO : HALO + ROWS, :]
    for tap in range(1, TAPS):
        total = total + taps_of(tap) * scratch[HALO - tap : HALO - tap + ROWS, :]
    return total.astype(BF16).astype(F32)


def front(lanes, sc, feats, cot, tail, head, cot_head, param, win, grad):
    capacity = cot.shape[0]
    shorts = []
    for m in range(3):
        fill(
            win.at[m], feats[m][:, lanes], tail[m][:, lanes], head[m][:, lanes], sc, capacity
        )
        shorts.append(
            short_conv(win.at[m], lambda tap, m=m: param[0, pl.ds(3 * tap + m, 1), lanes])
        )
    fill(grad, cot[:, lanes], None, cot_head[:, lanes], sc, capacity)
    query, key, value = shorts
    mixed = (key * value).astype(BF16).astype(F32)
    grad_rows = grad[HALO : HALO + ROWS, :]
    return query, key, value, mixed, grad_rows, grad_rows * query


def state_kernel(groups, sc, fq, fk, fv, cot, tq, tk, tv, hq, hk, hv, hc, param, out, wins, grad_wins):
    count = sc[0]

    def group(k):
        lanes = pl.ds(k * LANES, LANES)
        win, grad = wins.at[k], grad_wins.at[k]
        _, _, _, mixed, _, d_long = front(
            lanes, sc, (fq, fk, fv), cot, (tq, tk, tv), (hq, hk, hv), hc, param, win, grad
        )
        dec = column_of(param[0, DEC_ROW : DEC_ROW + 1, lanes])
        dec = jnp.concatenate([dec, dec], axis=1)
        step = iota((LANES, ROWS), 1)
        ahead = count - 1 - step
        powers = jnp.where(ahead >= 0, jnp.exp(-dec * jnp.maximum(ahead, 0).astype(F32)), 0.0)
        after = step - REACH
        inside = jnp.logical_and(after >= 0, after < count)
        back = jnp.where(inside, jnp.exp(-dec * jnp.maximum(after, 0).astype(F32)), 0.0)
        fwd = jnp.dot(powers.astype(BF16), mixed.astype(BF16), preferred_element_type=F32)
        bwd = jnp.dot(back.astype(BF16), d_long.astype(BF16), preferred_element_type=F32)
        same = same_filter()
        out[0, :, lanes] = fold(jnp.where(same, fwd, 0.0)).astype(BF16)
        out[1, :, lanes] = fold(jnp.where(same, bwd, 0.0)).astype(BF16)

    for k in range(groups):
        group(k)


def main_kernel(
    groups, shards, sc, fq, fk, fv, cot, tq, tk, tv, hq, hk, hv, hc, param, states,
    out, dfeat, dparam, wins, grad_wins, dshorts, dwin,
):
    count = sc[0]
    m_step = pl.program_id(1)
    capacity = cot.shape[0]

    def group(k):
        lanes = pl.ds(k * LANES, LANES)
        win, grad, dshort = wins.at[k], grad_wins.at[k], dshorts.at[k]
        query, key, value, mixed, grad_rows, d_long = front(
            lanes, sc, (fq, fk, fv), cot, (tq, tk, tv), (hq, hk, hv), hc, param, win, grad
        )
        row = iota((ROWS, LANES), 0)
        reach = row < count + REACH
        own = row < count
        mixed = jnp.where(reach, mixed, 0.0)
        d_long = jnp.where(reach, d_long, 0.0)
        d_own = jnp.where(own, d_long, 0.0)
        same = same_filter()
        res_row = param[0, RES_ROW : RES_ROW + 1, lanes]
        dec_row = param[0, DEC_ROW : DEC_ROW + 1, lanes]
        skip = param[0, SKIP_ROW : SKIP_ROW + 1, lanes]
        res = column_of(res_row)
        dec = column_of(dec_row)
        lane_f = iota((LANES, LANES), 1).astype(F32)
        sub_f = iota((LANES, LANES), 0).astype(F32)

        rate = fold(jnp.where(same, dec, 0.0))
        from_left = jnp.zeros((POLES, LANES), F32)
        from_right = jnp.zeros((POLES, LANES), F32)
        for i in range(shards):
            gap_l = sc[3 + i]
            gap_r = sc[3 + shards + i]
            gap = jnp.maximum(gap_l, gap_r)
            there = states[i, :, lanes].astype(F32)
            there = there * jnp.exp(-rate * jnp.maximum(gap, 0).astype(F32))
            from_left = from_left + jnp.where(gap_l >= 0, there, 0.0)
            from_right = from_right + jnp.where(gap_r >= 0, there, 0.0)

        pw_lag = jnp.exp(-dec * lane_f)
        turned = (iota((LANES, LANES), 1) * (LANES - 1)) % LANES
        pw_turn = jnp.exp(-dec * turned.astype(F32))
        k_lag = jnp.sum((res * pw_lag).reshape(PER, POLES, LANES), axis=1)
        k_turn = jnp.sum((res * pw_turn).reshape(PER, POLES, LANES), axis=1)
        lower = iota((BLK, BLK), 0) >= iota((BLK, BLK), 1)
        upper = iota((BLK, BLK), 0) <= iota((BLK, BLK), 1)

        def toeplitz(rows, keep):
            parts = []
            for f in range(PER):
                wide = jnp.broadcast_to(rows[f : f + 1, :], (BLK, LANES))
                wide = pltpu.roll(wide, 0, 1, stride=1, stride_axis=0)
                parts.append(jnp.where(keep, wide, 0.0).astype(BF16))
            return jnp.concatenate(parts, axis=1)

        t_fwd = toeplitz(k_turn, lower)
        t_bwd = toeplitz(k_lag, upper)

        def side(x):
            return jnp.concatenate([x[0:BLK], x[BLK:ROWS]], axis=1)

        def stacked(x):
            fil = lane_filter(2 * LANES)
            return jnp.concatenate(
                [jnp.where(fil == f, x, 0.0).astype(BF16) for f in range(PER)], axis=0
            )

        m_side = side(mixed)
        d_side = side(d_long)
        own_side = side(d_own).astype(BF16)
        mirror = iota((BLK, BLK), 0) + iota((BLK, BLK), 1)
        flip = jnp.where(mirror == BLK - 1, 1.0, 0.0).astype(BF16)
        own_flip = jnp.dot(flip, own_side, preferred_element_type=F32).astype(BF16)
        m_stack = stacked(m_side)
        d_stack = stacked(d_side)
        y_fwd = jnp.dot(t_fwd, m_stack, preferred_element_type=F32)
        y_bwd = jnp.dot(t_bwd, d_stack, preferred_element_type=F32)
        pair = lax.dot_general(
            own_flip, m_stack, (((1,), (1,)), ((), ())), preferred_element_type=F32
        )

        pw_rest = jnp.exp(-dec * (BLK - 1.0 - lane_f))
        in_pw = pw_rest.astype(BF16)
        out_pw = jnp.exp(-dec * (lane_f + 1.0)).astype(BF16)
        s_first = jnp.dot(in_pw, mixed[0:BLK].astype(BF16), preferred_element_type=F32)
        carry0 = unfold(from_left)
        carry1 = jnp.exp(-dec * float(BLK)) * carry0 + jnp.where(same, s_first, 0.0)
        carries = jnp.concatenate([carry0, carry1], axis=1)
        out_t = (res_row * jnp.exp(-dec_row * (sub_f + 1.0))).astype(BF16)
        y_fwd = y_fwd + jnp.dot(out_t, carries.astype(BF16), preferred_element_type=F32)
        seen = jnp.dot(out_pw, own_side, preferred_element_type=F32)

        e_second = jnp.dot(out_pw, d_long[BLK:ROWS].astype(BF16), preferred_element_type=F32)
        e_second = jnp.where(same, e_second, 0.0).astype(BF16)
        in_t = (res_row * jnp.exp(-dec_row * (BLK - 1.0 - sub_f))).astype(BF16)
        until = jnp.maximum(count + REACH - row, 0).astype(F32)
        far_t = (res_row * jnp.exp(-dec_row * until)).astype(BF16)
        y_far = jnp.dot(far_t, unfold(from_right).astype(BF16), preferred_element_type=F32)
        y_near = jnp.dot(in_t, e_second, preferred_element_type=F32)

        long_out = jnp.concatenate([y_fwd[:, 0:LANES], y_fwd[:, LANES:]], axis=0) + skip * mixed
        d_mixed = (
            jnp.concatenate([y_bwd[:, 0:LANES] + y_near, y_bwd[:, LANES:]], axis=0)
            + y_far
            + skip * d_long
        )
        gated = jnp.where(own, query * long_out, 0.0)
        out[:, lanes] = gated[0:capacity].astype(BF16)

        lag_rows = []
        for f in range(PER):
            piece = jnp.where(mirror < BLK, pair[:, f * LANES : (f + 1) * LANES], 0.0)
            piece = pltpu.roll(piece, 0, 1, stride=1, stride_axis=0)
            lag_rows.append(jnp.broadcast_to(jnp.sum(piece, axis=0, keepdims=True), (POLES, LANES)))
        lag_sums = jnp.concatenate(lag_rows, axis=0)
        crossed = seen * carries
        res_grad = lag_sums * pw_rest + crossed[:, 0:LANES] + crossed[:, LANES:]
        dparam[RES_ROW : RES_ROW + 1, lanes] = jnp.sum(
            jnp.transpose(res_grad), axis=0, keepdims=True
        )
        dparam[SKIP_ROW : SKIP_ROW + 1, lanes] = jnp.sum(d_own * mixed, axis=0, keepdims=True)

        d_parts = (grad_rows * long_out, d_mixed * value, d_mixed * key)
        for m in range(3):
            d_m = jnp.where(reach, d_parts[m], 0.0)
            dshort[0:ROWS, :] = d_m
            d_m = jnp.where(own, d_m, 0.0)
            total = jnp.zeros((capacity, LANES), F32)
            for tap in range(TAPS):
                weight = param[0, 3 * tap + m : 3 * tap + m + 1, lanes]
                total = total + weight * dshort[tap : tap + capacity, :]
                piece = d_m * win[m, HALO - tap : HALO - tap + ROWS, :]
                dparam[3 * tap + m : 3 * tap + m + 1, lanes] = jnp.sum(
                    piece, axis=0, keepdims=True
                )
            dwin[m, :, lanes] = jnp.where(own[0:capacity], total, 0.0).astype(BF16)

    @pl.when(m_step == 0)
    def _():
        dparam[GRAD_ROWS - 1 : GRAD_ROWS, :] = jnp.zeros((1, dparam.shape[1]), F32)
        dshorts[:, ROWS:, :] = jnp.zeros((groups, dshorts.shape[1] - ROWS, LANES), F32)
        for k in range(groups):
            group(k)

    dfeat[...] = dwin[m_step]


MESH = pl.DeviceIdType.MESH


def meet(peers):
    barrier = pltpu.get_barrier_semaphore()
    for peer in peers:
        pl.semaphore_signal(barrier, inc=1, device_id=peer, device_id_type=MESH)
    pl.semaphore_wait(barrier, len(peers))


def params_kernel(shards, packed, tail, head, params, tail_in, head_in, send, recv, own):
    dp, me = lax.axis_index("dp"), lax.axis_index("ctx")
    peers = [(dp, lax.rem(me + d, shards)) for d in range(1, shards)]
    meet(peers)
    local = pltpu.make_async_copy(packed, params.at[me], own)
    local.start()
    jobs = [(tail, tail_in, peers[0]), (head, head_in, peers[-1])]
    jobs += [(packed, params.at[me], peer) for peer in peers]
    copies = []
    for n, (src, dst, peer) in enumerate(jobs):
        copies.append(
            pltpu.make_async_remote_copy(
                src_ref=src, dst_ref=dst, send_sem=send.at[n], recv_sem=recv.at[n],
                device_id=peer, device_id_type=MESH,
            )
        )
        copies[-1].start()
    local.wait()
    for copy in copies:
        copy.wait()


def spread_kernel(shards, states, seen, send, recv):
    dp, me = lax.axis_index("dp"), lax.axis_index("ctx")
    peers = [(dp, lax.rem(me + d, shards)) for d in range(1, shards)]
    meet(peers)
    copies = []
    for n, peer in enumerate(peers):
        way = (peer[1] < me).astype(jnp.int32)
        copies.append(
            pltpu.make_async_remote_copy(
                src_ref=states.at[way], dst_ref=seen.at[me], send_sem=send.at[n],
                recv_sem=recv.at[n], device_id=peer, device_id_type=MESH,
            )
        )
        copies[-1].start()
    for copy in copies:
        copy.wait()


def reduce_kernel(shards, replicas, part, out, by_ctx, by_dp, send, recv, send_dp, recv_dp):
    dp, me = lax.axis_index("dp"), lax.axis_index("ctx")
    chan = out.shape[1]
    peers = [(dp, lax.rem(me + d, shards)) for d in range(1, shards)]
    others = [(lax.rem(dp + d, replicas), me) for d in range(1, replicas)]
    meet(peers + others)
    copies = []
    for n, peer in enumerate(peers):
        lanes = pl.ds(pl.multiple_of(peer[1] * chan, LANES), chan)
        copies.append(
            pltpu.make_async_remote_copy(
                src_ref=part.at[:, lanes], dst_ref=by_ctx.at[n], send_sem=send.at[n],
                recv_sem=recv.at[n], device_id=peer, device_id_type=MESH,
            )
        )
        copies[-1].start()
    total = part[:, pl.ds(pl.multiple_of(me * chan, LANES), chan)]
    for n, copy in enumerate(copies):
        copy.wait()
        total = total + by_ctx[n]
    by_dp[dp] = total
    copies = []
    for n, peer in enumerate(others):
        copies.append(
            pltpu.make_async_remote_copy(
                src_ref=by_dp.at[dp], dst_ref=by_dp.at[dp], send_sem=send_dp.at[n],
                recv_sem=recv_dp.at[n], device_id=peer, device_id_type=MESH,
            )
        )
        copies[-1].start()
    for copy in copies:
        copy.wait()
    total = by_dp[0]
    for n in range(1, replicas):
        total = total + by_dp[n]
    out[...] = total


def remote(ident):
    return pltpu.CompilerParams(collective_id=ident, has_side_effects=True)


def per_device(features, counts, short_taps, residue, decay_rate, skip_gain, cotangent):
    shards = lax.axis_size("ctx")
    me = lax.axis_index("ctx")
    capacity = features.shape[2]
    width = cotangent.shape[3]
    chan = short_taps.shape[2]
    groups = chan // LANES
    feats = features[0, 0]
    cot = cotangent[0, 0]
    count = counts[0, 0]

    packed = jnp.concatenate(
        [
            short_taps.reshape(3 * TAPS, chan),
            skip_gain.reshape(1, chan),
            residue.T.reshape(1, chan),
            decay_rate.T.reshape(1, chan),
            jnp.broadcast_to(count.astype(F32), (PARAM_ROWS - CNT_ROW, chan)),
        ],
        axis=0,
    )
    tail = lax.dynamic_slice(feats, (count - HALO, 0), (HALO, 3 * width))
    head = jnp.concatenate([feats[0:HALO], cot[0:HALO]], axis=1)
    anywhere = pl.BlockSpec(memory_space=pl.ANY)
    params, tail, head = pl.pallas_call(
        functools.partial(params_kernel, shards),
        in_specs=[anywhere] * 3,
        out_specs=[anywhere] * 3,
        out_shape=[
            jax.ShapeDtypeStruct((shards,) + packed.shape, F32),
            jax.ShapeDtypeStruct(tail.shape, BF16),
            jax.ShapeDtypeStruct(head.shape, BF16),
        ],
        scratch_shapes=[
            pltpu.SemaphoreType.DMA((shards + 1,)),
            pltpu.SemaphoreType.DMA((shards + 1,)),
            pltpu.SemaphoreType.DMA,
        ],
        compiler_params=remote(0),
        name="params",
    )(packed, tail, head)

    all_counts = params[:, CNT_ROW, 0].astype(jnp.int32)
    ends = jnp.cumsum(all_counts)
    starts = ends - all_counts
    ids = jnp.arange(shards, dtype=jnp.int32)
    gap_l = jnp.where(ids < me, starts[me] - ends, -1)
    gap_r = jnp.where(ids > me, starts - ends[me], -1)
    edges = jnp.stack([me > 0, me < shards - 1]).astype(jnp.int32)
    scalars = jnp.concatenate([count[None], edges, gap_l, gap_r]).astype(jnp.int32)

    def cols(rows, offset):
        return pl.BlockSpec((rows, chan), lambda g, *_: (0, offset * shards + g))

    smem = pl.BlockSpec(memory_space=pltpu.SMEM)
    specs = [smem]
    specs += [cols(capacity, m) for m in range(3)] + [cols(capacity, 0)]
    specs += [cols(HALO, m) for m in range(3)] + [cols(HALO, m) for m in range(4)]
    specs += [pl.BlockSpec((1, PARAM_ROWS, chan), lambda g, *_: (g, 0, 0))]
    args = [scalars, feats, feats, feats, cot, tail, tail, tail, head, head, head, head, params]
    ext = HALO + ROWS + HALO
    states = pl.pallas_call(
        functools.partial(state_kernel, groups),
        grid=(shards,),
        in_specs=specs,
        out_specs=pl.BlockSpec((2, POLES, chan), lambda g: (0, 0, g)),
        out_shape=jax.ShapeDtypeStruct((2, POLES, width), BF16),
        scratch_shapes=[pltpu.VMEM((groups, 3, ext, LANES), F32), pltpu.VMEM((groups, ext, LANES), F32)],
        name="states",
    )(*args)
    states = pl.pallas_call(
        functools.partial(spread_kernel, shards),
        in_specs=[anywhere],
        out_specs=anywhere,
        out_shape=jax.ShapeDtypeStruct((shards, POLES, width), BF16),
        scratch_shapes=[
            pltpu.SemaphoreType.DMA((shards - 1,)),
            pltpu.SemaphoreType.DMA((shards - 1,)),
        ],
        compiler_params=remote(1),
        name="spread",
    )(states)

    out, dfeat, dparam = pl.pallas_call(
        functools.partial(main_kernel, groups, shards),
        grid=(shards, 3),
        in_specs=specs + [pl.BlockSpec((shards, POLES, chan), lambda g, *_: (0, 0, g))],
        out_specs=[
            cols(capacity, 0),
            pl.BlockSpec((capacity, chan), lambda g, m: (0, m * shards + g)),
            cols(GRAD_ROWS, 0),
        ],
        out_shape=[
            jax.ShapeDtypeStruct((capacity, width), BF16),
            jax.ShapeDtypeStruct((capacity, 3 * width), BF16),
            jax.ShapeDtypeStruct((GRAD_ROWS, width), F32),
        ],
        scratch_shapes=[
            pltpu.VMEM((groups, 3, ext, LANES), F32),
            pltpu.VMEM((groups, ext, LANES), F32),
            pltpu.VMEM((groups, ROWS + HALO, LANES), F32),
            pltpu.VMEM((3, capacity, chan), BF16),
        ],
        name="main",
    )(*args, states)
    replicas = lax.axis_size("dp")
    vmem = pl.BlockSpec(memory_space=pltpu.VMEM)
    grads = pl.pallas_call(
        functools.partial(reduce_kernel, shards, replicas),
        in_specs=[vmem],
        out_specs=vmem,
        out_shape=jax.ShapeDtypeStruct((GRAD_ROWS, chan), F32),
        scratch_shapes=[
            pltpu.VMEM((shards - 1, GRAD_ROWS, chan), F32),
            pltpu.VMEM((replicas, GRAD_ROWS, chan), F32),
            pltpu.SemaphoreType.DMA((shards - 1,)),
            pltpu.SemaphoreType.DMA((shards - 1,)),
            pltpu.SemaphoreType.DMA((replicas - 1,)),
            pltpu.SemaphoreType.DMA((replicas - 1,)),
        ],
        compiler_params=remote(2),
        name="reduce",
    )(dparam)
    return (
        out[None, None],
        dfeat[None, None],
        grads[0 : 3 * TAPS].reshape(TAPS, 3, chan),
        grads[RES_ROW].reshape(chan // GROUP, POLES).T,
        grads[SKIP_ROW],
    )


def solution(mesh):
    in_specs = (
        P("dp", "ctx", None, None),
        P("dp", "ctx"),
        P(None, None, "ctx"),
        P(None, "ctx"),
        P(None, "ctx"),
        P("ctx"),
        P("dp", "ctx", None, None),
    )
    out_specs = (
        P("dp", "ctx", None, None),
        P("dp", "ctx", None, None),
        P(None, None, "ctx"),
        P(None, "ctx"),
        P("ctx"),
    )
    return jax.shard_map(
        per_device, mesh=mesh, in_specs=in_specs, out_specs=out_specs, check_vma=False
    )
```
